32 devices in a mesh: tile: 8 (over y, x, core), mem: 4 (over z).
Axes of the slice: x: 2, y: 2, z: 4, core: 2. Of those that a mesh axis runs over, the one named last changes fastest.
Arguments:
- velocity: bfloat16 [96, 2, 8, 32768], P('mem', None, None, 'tile'), may hold values from -6 to 6
- start_frac: float32 [2, 16384], P(None, 'tile'), may hold values from 0 to 1
- observed: float32 [2, 16384], P(None, 'tile'), may hold values from -0.5 to 1.5
- obs_sd: float32 [16384], P('tile'), may hold values from 0.3 to 3
- tile_of: int32 [16384, 1], P('tile'), may hold values from 0 to 7; in each aligned block of 2048 rows (0 to 2047, 2048 to 4095, ...) at most 512 rows name the same one
- cell_of: int32 [16384], P('tile'), may hold values from 0 to 4030, as said below
Outputs:
- analysis_velocity: bfloat16 [96, 2, 8, 32768], P('mem', None, None, 'tile')
- analysis_positions: float32 [96, 2, 16384], P('mem', None, 'tile')
The draws below stay inside these ranges and needn't reach their ends.
Inputs may be any that keep to these rules, and one draw needn't show every extreme that they name: cell_of is i * 64 + j with i and j below 63, so the stencil's four cells lie in the same tile. `tile_of`: of the drifters of one index of tile, at most 512 name one tile, a bound that some block reaches of them.
All inputs are finite; a program needn't handle non-finite values.
Results may differ from the reference program's by a relative error of at most 0.0048.
Values may be sent and summed in bfloat16 or wider, within the bound.
No kernel may reach another device: no remote copies, remote signals or barrier semaphores. Data moves between devices by JAX's collectives and lax.ppermute only.
A program may use at most 64 MiB of HBM per device.

```python
import math
import jax
import jax.numpy as jnp
import numpy as np
from jax import lax

MEMBERS = 96
LEVELS = 8
BX = 64
P_DEV = 2048
CELLS = 4096
CELLS_ALL = 32768
DRIFTERS = 16384
CAP = 512
N_TILE = 8


def draw_cell_of(key, part):
    row_index = jax.random.randint(jax.random.fold_in(key, 11), (DRIFTERS,), 0, BX - 1)
    col_index = jax.random.randint(jax.random.fold_in(key, 12), (DRIFTERS,), 0, BX - 1)
    return (row_index * BX + col_index).astype(jnp.int32)


def level_of(stream_key, extent, pieces, low, top_value):
    loudness, own = 1.0, jax.random.fold_in(stream_key, 6)
    for dim, parts in pieces:
        draws = jnp.exp(jax.random.uniform(jax.random.fold_in(own, dim), (parts,), jnp.float32, low / len(pieces), top_value / len(pieces)))
        loudness = loudness * jnp.repeat(draws, extent[dim] // parts).reshape([-1 if axis == dim else 1 for axis in range(len(extent))])
    return loudness


def assign_block(rng, own, number, rows, amount, top, limit, lean):
    sequence = jax.random.permutation(rng, amount)
    heavy_load, ordinary = portions_of(amount, rows * top, limit, lean, True), portions_of(amount, rows * top, limit, lean, False)
    places = jnp.arange(amount)

    def named(lengths, offset_by):
        used = int((lengths > 0).sum())
        fixed = max(1, used // 4)
        moved = fixed + (places - fixed + offset_by * (used - fixed)) % max(1, amount - fixed)
        return jnp.zeros((amount,), jnp.int32).at[sequence[jnp.where(places < fixed, places, moved)]].set(jnp.asarray(lengths, jnp.int32))

    lengths = jnp.where(number % 4 == 0, named(heavy_load, number // 4), named(ordinary, number - number // 4 - 1))
    mixed = jax.random.permutation(jax.random.fold_in(own, 3), amount)
    giver, receiver = mixed[0:amount // 2 * 2:2], mixed[1:amount // 2 * 2:2]
    room = jnp.minimum(lengths[giver] - 1, limit - lengths[receiver]) // 2
    room = jnp.where((giver == sequence[0]) | (receiver == sequence[0]) | (lengths[receiver] == 0), 0, jnp.maximum(room, 0))
    moved = jax.random.randint(jax.random.fold_in(own, 4), (amount // 2,), 0, 1 << 20) % (room + 1)
    lengths = lengths.at[giver].add(-moved).at[receiver].add(moved)
    items = jnp.searchsorted(jnp.cumsum(lengths), jnp.arange(rows * top), side="right").astype(jnp.int32)
    listing = items.reshape(top, rows).T
    listing = listing[jax.random.permutation(jax.random.fold_in(own, 1), rows)]
    offset_by = jax.random.randint(jax.random.fold_in(own, 2), (rows, 1), 0, top)
    return jnp.take_along_axis(listing, (jnp.arange(top)[None, :] + offset_by) % top, axis=1)


def portions_of(number_of, total, reach, skew, full):
    portions = [(1 << 20) // math.isqrt(standing ** skew) + 1 for standing in range(1, number_of + 1)]
    largest = reach if full else min(reach, max(-(-total // number_of), total * portions[0] // sum(portions)))
    least = 1 if total - largest >= number_of - 1 else 0
    holding, surplus = [largest] + [least] * (number_of - 1), total - largest - least * (number_of - 1)
    while surplus > 0:
        candidates = [i for i in range(1, number_of) if holding[i] < largest] or [i for i in range(1, number_of) if holding[i] < reach]
        pool, remaining = sum([portions[i] for i in candidates]), surplus
        for i in candidates:
            extra = min(reach - holding[i], max(1, remaining * portions[i] // pool), surplus)
            holding[i] = holding[i] + extra
            surplus = surplus - extra
    return np.array(holding)


def normal_values(stream_key, extent, width, reach, shards=(), kind=jnp.bfloat16):
    values = jax.random.normal(stream_key, extent, jnp.float32) * width
    if len(shards) > 0:
        values = level_of(stream_key, extent, shards, -0.22, 0.18) * values
    return jnp.clip(values, min=-reach, max=reach).astype(kind)


def setup_inputs(seed: int = 0) -> dict:
    keys = jax.random.split(jax.random.key(seed), 7)
    velocity = normal_values(keys[0], (MEMBERS, 2, LEVELS, CELLS_ALL), 1.0, 6.0, ((0, 4), (3, 8)))
    start_frac = jnp.clip(1.0 * jax.random.uniform(keys[1], (2, DRIFTERS), jnp.float32) ** level_of(keys[1], (2, DRIFTERS), ((1, 8),), -0.2, 0.2), 0.0, 1.0)
    observed = jnp.clip(-0.5 + 2.0 * jax.random.uniform(keys[2], (2, DRIFTERS), jnp.float32) ** level_of(keys[2], (2, DRIFTERS), ((1, 8),), -0.2, 0.2), -0.5, 1.5)
    obs_sd = jnp.clip(jnp.exp(math.log(3.0) - 2.3025851 * jax.random.uniform(keys[3], (DRIFTERS,), jnp.float32) ** level_of(keys[3], (DRIFTERS,), ((0, 8),), -0.2, 0.2)), 0.3, 3.0)
    tile_of_keys = jax.random.split(jax.random.fold_in(keys[4], 1), DRIFTERS // P_DEV)
    tile_of_turns = jax.random.permutation(jax.random.fold_in(keys[4], 3), DRIFTERS // P_DEV)
    tile_of = jax.vmap(lambda own, number: assign_block(jax.random.fold_in(keys[4], 2), own, number, P_DEV, N_TILE, 1, CAP, 2))(tile_of_keys, tile_of_turns).reshape((DRIFTERS, 1))
    cell_of = draw_cell_of(jax.random.fold_in(keys[6], 71), 0)
    return {"velocity": velocity, "start_frac": start_frac, "observed": observed, "obs_sd": obs_sd, "tile_of": tile_of, "cell_of": cell_of}


step_dt = 0.2

def bilinear(corner, position):
    frac_x = position[:, 0:1, :]
    frac_y = position[:, 1:2, :]
    return (1.0 - frac_x) * (1.0 - frac_y) * corner[0] + frac_x * (1.0 - frac_y) * corner[1] + (1.0 - frac_x) * frac_y * corner[2] + frac_x * frac_y * corner[3]

def advect(corner, start):
    position = jnp.broadcast_to(start[None], corner[0].shape)
    for repeat in range(2):
        slope_one = bilinear(corner, position)
        midway = position + 0.5 * step_dt * slope_one
        slope_two = bilinear(corner, midway)
        position = position + step_dt * slope_two
    return position

def ensemble_weights(gram_matrix, projection):
    members = gram_matrix.shape[0]
    identity = jnp.eye(members, dtype=jnp.float32)
    factor = jnp.linalg.cholesky(identity + gram_matrix)
    half_solve = lax.linalg.triangular_solve(factor, projection[:, None], left_side=True, lower=True)
    mean_weight = lax.linalg.triangular_solve(factor, half_solve, left_side=True, lower=True, transpose_a=True)
    inverse_root = lax.linalg.triangular_solve(factor, identity, left_side=True, lower=True, transpose_a=True)
    combined = mean_weight + jnp.sqrt(jnp.float32(members - 1)) * inverse_root
    return combined - lax.optimization_barrier(jnp.mean(combined, axis=0, keepdims=True)) + 1.0 / members

def reference(velocity, start_frac, observed, obs_sd, tile_of, cell_of):
    level_zero = velocity[:, :, 0, :].astype(jnp.float32)
    flat_index = (tile_of[:, 0] * CELLS + cell_of).astype(jnp.int32)
    offsets = (0, 1, BX, BX + 1)
    corner = jnp.stack([jnp.take(level_zero, flat_index + shift_by, axis=2) for shift_by in offsets], 0)
    predicted = advect(corner, start_frac)
    ens_mean = lax.optimization_barrier(jnp.mean(predicted, axis=0))
    inverse_scale = 1.0 / (obs_sd * jnp.sqrt(jnp.float32(MEMBERS - 1)))
    anomaly = ((predicted - ens_mean[None]) * inverse_scale).reshape(MEMBERS, -1)
    innovation = ((observed - ens_mean) / obs_sd).reshape(-1)
    gram_matrix = jnp.dot(anomaly, anomaly.T, precision=lax.Precision.HIGHEST)
    projection = jnp.dot(anomaly, innovation, precision=lax.Precision.HIGHEST)
    weights = ensemble_weights(gram_matrix, projection)
    new_positions = jnp.dot(weights.T, predicted.reshape(MEMBERS, -1), precision=lax.Precision.HIGHEST)
    weights_bf = weights.astype(jnp.bfloat16)
    layers = []
    for component in range(2):
        for level in range(LEVELS):
            layers.append(jnp.dot(weights_bf.T.astype(jnp.float32), velocity[:, component, level, :].astype(jnp.float32), preferred_element_type=jnp.float32).astype(jnp.bfloat16))
    new_velocity = jnp.stack(layers, 1).reshape(MEMBERS, 2, LEVELS, -1)
    return (new_velocity, new_positions.reshape(MEMBERS, 2, -1))
```

```python
import functools
import math

import jax
import jax.numpy as jnp
from jax import lax
from jax.experimental import pallas as pl
from jax.experimental.pallas import tpu as pltpu
from jax.sharding import PartitionSpec as P

BX = 64
LANES = 128
STEP = 0.2
BF16 = jnp.bfloat16
F32 = jnp.float32
I32 = jnp.int32
HIGHEST = lax.Precision.HIGHEST
NT = (((1,), (1,)), ((), ()))


def iota(shape, dim):
    return lax.broadcasted_iota(I32, shape, dim)


def quotient(values, divisor):
    return ((values.astype(F32) + 0.5) * (1.0 / divisor)).astype(I32)


def ones_where(mask, dtype=BF16):
    return jnp.where(mask, 1.0, 0.0).astype(dtype)


def vmem():
    return pl.BlockSpec(memory_space=pltpu.VMEM)


def pack_kernel(local, levels, share, v_ref, halo_ref, zero_ref, rest0_ref, rest1_ref):
    rows = v_ref.shape[0]
    i = iota((2 * local, rows), 0)
    j = iota((2 * local, rows), 1)
    comp = (i >= local).astype(I32)
    pick = ones_where(j == ((i - comp * local) * 2 + comp) * levels)
    x = v_ref[...]
    zero_ref[0, :, :share] = jnp.dot(pick, x, preferred_element_type=F32).astype(BF16)
    zero_ref[0, :, share:] = jnp.dot(pick, halo_ref[...], preferred_element_type=F32).astype(BF16)
    other = levels - 1
    i = iota((other * local, rows), 0)
    j = iota((other * local, rows), 1)
    member = quotient(i, other)
    base = member * 2 * levels + (i - member * other) + 1
    for c, ref in enumerate((rest0_ref, rest1_ref)):
        pick = ones_where(j == base + c * levels)
        ref[0] = jnp.dot(pick, x, preferred_element_type=F32).astype(BF16)


def pack(velocity, shares):
    local, _, levels, cells = velocity.shape
    share = cells // shares
    rows = local * 2 * levels
    flat = velocity.reshape(rows, cells)
    steps = share // LANES
    last = cells // LANES - 1
    other = (levels - 1) * local
    return pl.pallas_call(
        functools.partial(pack_kernel, local, levels, share),
        grid=(shares,),
        in_specs=[
            pl.BlockSpec((rows, share), lambda q: (0, q)),
            pl.BlockSpec((rows, LANES), lambda q: (0, jnp.minimum((q + 1) * steps, last))),
        ],
        out_specs=[
            pl.BlockSpec((1, 2 * local, share + LANES), lambda q: (q, 0, 0)),
            pl.BlockSpec((1, other, share), lambda q: (q, 0, 0)),
            pl.BlockSpec((1, other, share), lambda q: (q, 0, 0)),
        ],
        out_shape=[
            jax.ShapeDtypeStruct((shares, 2 * local, share + LANES), BF16),
            jax.ShapeDtypeStruct((shares, other, share), BF16),
            jax.ShapeDtypeStruct((shares, other, share), BF16),
        ],
        name="pack",
    )(flat, flat)


def route_kernel(tiles, blocks, share, q_ref, tile_ref, cell_ref, frac_ref, obs_ref, sd_ref, req_ref, where_ref, count_ref):
    drifters = cell_ref.shape[1]
    dest = tile_ref[...]
    local_cell = cell_ref[...] - q_ref[0] * share
    mine = jnp.logical_and(local_cell >= 0, local_cell < share)
    named = jnp.where(jnp.logical_and(iota((tiles, drifters), 0) == dest, mine), 1.0, 0.0)
    upper = ones_where(iota((LANES, LANES), 0) <= iota((LANES, LANES), 1))
    before = jnp.zeros((tiles, 1), F32)
    sums = []
    for start in range(0, drifters, LANES):
        part = named[:, start : start + LANES]
        sums.append(jnp.dot(part.astype(BF16), upper, preferred_element_type=F32) + before)
        before = before + jnp.sum(part, axis=1, keepdims=True)
    running = jnp.concatenate(sums, axis=1)
    slot = jnp.sum(named * (running - 1.0), axis=0, keepdims=True).astype(I32)
    total = jnp.sum(named * before, axis=0, keepdims=True)
    where_to = jnp.where(mine, dest * (blocks * LANES) + slot, -1)
    where_ref[...] = where_to
    count_ref[...] = jnp.broadcast_to(before, count_ref.shape)
    payload = jnp.concatenate(
        [local_cell.astype(F32), frac_ref[...], obs_ref[...], sd_ref[...], jnp.ones_like(total), total], axis=0
    )
    high = lax.shift_right_arithmetic(where_to, int(math.log2(LANES)))
    low = jnp.bitwise_and(where_to, LANES - 1)
    spread = jnp.concatenate([jnp.where(high == h, payload, 0.0) for h in range(tiles * blocks)], axis=0)
    place = ones_where(iota((LANES, drifters), 0) == low, F32)
    placed = lax.dot_general(spread, place, NT, precision=HIGHEST, preferred_element_type=F32)
    per = 8 * blocks
    for t in range(tiles):
        req_ref[t] = placed[t * per : (t + 1) * per]


def route(q, tile_of, cell_of, start_frac, observed, obs_sd, tiles, blocks, share):
    drifters = cell_of.shape[0]
    return pl.pallas_call(
        functools.partial(route_kernel, tiles, blocks, share),
        in_specs=[pl.BlockSpec(memory_space=pltpu.SMEM)] + [vmem()] * 5,
        out_specs=[vmem()] * 3,
        out_shape=[
            jax.ShapeDtypeStruct((tiles, 8 * blocks, LANES), F32),
            jax.ShapeDtypeStruct((1, drifters), I32),
            jax.ShapeDtypeStruct((tiles, LANES), F32),
        ],
        name="route",
    )(
        q.reshape(1),
        tile_of.reshape(1, drifters),
        cell_of.reshape(1, drifters),
        start_frac,
        observed,
        obs_sd.reshape(1, drifters),
    )


def bilinear(corner, x, y):
    return (1.0 - x) * (1.0 - y) * corner[0] + x * (1.0 - y) * corner[1] + (1.0 - x) * y * corner[2] + x * y * corner[3]


def block_count(value):
    return lax.shift_right_arithmetic(jnp.max(value).astype(I32) + (LANES - 1), int(math.log2(LANES)))


def observe_kernel(members, local, zero_ref, req_ref, pred_ref, gram_ref, table_ref, corner_ref):
    sources = req_ref.shape[0]
    rows, width = zero_ref.shape
    i = iota((rows, rows), 0)
    j = iota((rows, rows), 1)
    comp = (i >= members).astype(I32)
    member = i - comp * members
    source = quotient(member, local)
    pick = ones_where(j == source * 2 * local + comp * local + member - source * local)
    table = jnp.dot(pick, zero_ref[...], preferred_element_type=F32)
    for n, offset in enumerate((0, 1, BX, BX + 1)):
        moved = table if offset == 0 else pltpu.roll(table, width - offset, 1)
        table_ref[n * rows : (n + 1) * rows, :] = moved.astype(BF16)
    gram_ref[...] = jnp.zeros_like(gram_ref)
    spread = math.sqrt(members - 1)

    def one_block(s, b):
        r = req_ref[s, pl.ds(pl.multiple_of(b * 8, 8), 8), :]
        cell = r[0:1].astype(I32)
        hit = ones_where(iota((width, LANES), 0) == cell)
        corner_ref[...] = jnp.dot(table_ref[...], hit, preferred_element_type=F32)
        cx = [corner_ref[n * rows : n * rows + members, :] for n in range(4)]
        cy = [corner_ref[n * rows + members : (n + 1) * rows, :] for n in range(4)]
        x = jnp.broadcast_to(r[1:2], (members, LANES))
        y = jnp.broadcast_to(r[2:3], (members, LANES))
        for _ in range(2):
            mx = x + 0.5 * STEP * bilinear(cx, x, y)
            my = y + 0.5 * STEP * bilinear(cy, x, y)
            x = x + STEP * bilinear(cx, mx, my)
            y = y + STEP * bilinear(cy, mx, my)
        lanes = pl.ds(pl.multiple_of(b * LANES, LANES), LANES)
        pred_ref[s, 0:members, lanes] = x
        pred_ref[s, members:rows, lanes] = y
        valid = r[6:7] > 0.5
        deviation = jnp.where(valid, r[5:6], 1.0)
        scale = jnp.where(valid, 1.0 / (deviation * spread), 0.0)
        inverse = jnp.where(valid, 1.0 / deviation, 0.0)
        mean_x = jnp.sum(x, axis=0, keepdims=True) * (1.0 / members)
        mean_y = jnp.sum(y, axis=0, keepdims=True) * (1.0 / members)
        anomaly = jnp.concatenate([(x - mean_x) * scale, (y - mean_y) * scale], axis=1)
        innovation = jnp.concatenate([(r[3:4] - mean_x) * inverse, (r[4:5] - mean_y) * inverse], axis=1)
        first = iota((8, 2 * LANES), 0) == 0
        both = jnp.concatenate([anomaly, jnp.where(first, innovation, 0.0)], axis=0)
        gram_ref[:, 0 : members + 8] += lax.dot_general(anomaly, both, NT, precision=HIGHEST, preferred_element_type=F32)

    def one_source(s, carry):
        amount = block_count(req_ref[s, 7:8, :])
        lax.fori_loop(0, amount, lambda b, c: (one_block(s, b), c)[1], 0)
        return carry

    lax.fori_loop(0, sources, one_source, 0)


def observe(zero, requests, members, local):
    sources, per, _ = requests.shape
    rows, width = zero.shape
    return pl.pallas_call(
        functools.partial(observe_kernel, members, local),
        in_specs=[vmem()] * 2,
        out_specs=[vmem()] * 2,
        out_shape=[
            jax.ShapeDtypeStruct((sources, rows, per // 8 * LANES), F32),
            jax.ShapeDtypeStruct((members, LANES), F32),
        ],
        scratch_shapes=[pltpu.VMEM((4 * rows, width), BF16), pltpu.VMEM((4 * rows, LANES), F32)],
        name="observe",
    )(zero, requests)


def all_sum(x):
    for axis in ("tile", "mem"):
        size = lax.axis_size(axis)
        bit = 1
        while bit < size:
            if size // bit >= 4 and not (axis == "tile" and bit == 1):
                a, b, c = [lax.ppermute(x, axis, [(n, n ^ (bit * k)) for n in range(size)]) for k in (1, 2, 3)]
                x = (x + a) + (b + c)
                bit *= 4
            else:
                x = x + lax.ppermute(x, axis, [(n, n ^ bit) for n in range(size)])
                bit *= 2
    return x


def ensemble_weights(gram_matrix, projection):
    members = gram_matrix.shape[0]
    identity = jnp.eye(members, dtype=F32)
    factor = jnp.linalg.cholesky(identity + gram_matrix)
    half_solve = lax.linalg.triangular_solve(factor, projection[:, None], left_side=True, lower=True)
    mean_weight = lax.linalg.triangular_solve(factor, half_solve, left_side=True, lower=True, transpose_a=True)
    inverse_root = lax.linalg.triangular_solve(factor, identity, left_side=True, lower=True, transpose_a=True)
    combined = mean_weight + jnp.sqrt(F32(members - 1)) * inverse_root
    return combined - jnp.mean(combined, axis=0, keepdims=True) + 1.0 / members


def spread_kernel(members, local, levels, w_ref, rest_ref, zero0_ref, zero1_ref, pos_ref):
    other = levels - 1
    weights = w_ref[...]
    rows = members * levels
    i = iota((rows, members), 0)
    repeat = ones_where(quotient(i, levels) == iota((rows, members), 1))
    tall = lax.dot_general(repeat, weights.astype(BF16), NT, preferred_element_type=F32).astype(BF16)
    cols = members * other
    j = iota((members, cols), 1)
    k = iota((members, cols), 0)
    widen = ones_where(jnp.logical_and(j >= k * other, j < (k + 1) * other))
    wide = jnp.dot(tall, widen, preferred_element_type=F32)
    i = iota((rows, cols), 0)
    j = iota((rows, cols), 1)
    same = i - quotient(i, levels) * levels == j - quotient(j, other) * other + 1
    rest_ref[...] = jnp.where(same, wide, 0.0).astype(BF16)
    j = iota((members, 2 * members), 1)
    k = iota((members, 2 * members), 0)
    source = quotient(k, local)
    i = iota((rows, 2 * members), 0)
    level0 = i - quotient(i, levels) * levels == 0
    for c, ref in enumerate((zero0_ref, zero1_ref)):
        move = ones_where(j == source * 2 * local + c * local + k - source * local)
        ref[...] = jnp.where(level0, jnp.dot(tall, move, preferred_element_type=F32), 0.0).astype(BF16)
    i = iota((2 * members, members), 0)
    half = quotient(i, 2)
    repeat = ones_where(half == iota((2 * members, members), 1), F32)
    tall = lax.dot_general(repeat, weights, NT, precision=HIGHEST, preferred_element_type=F32)
    odd = i - 2 * half == 1
    pos_ref[:, :members] = jnp.where(odd, 0.0, tall)
    pos_ref[:, members:] = jnp.where(odd, tall, 0.0)


def spread_weights(weights, local, levels):
    members = weights.shape[0]
    rows = members * levels
    return pl.pallas_call(
        functools.partial(spread_kernel, members, local, levels),
        in_specs=[vmem()],
        out_specs=[vmem()] * 4,
        out_shape=[
            jax.ShapeDtypeStruct((rows, members * (levels - 1)), BF16),
            jax.ShapeDtypeStruct((rows, 2 * members), BF16),
            jax.ShapeDtypeStruct((rows, 2 * members), BF16),
            jax.ShapeDtypeStruct((2 * members, 2 * members), F32),
        ],
        name="spread",
    )(weights)


def mix_kernel(share, rest_ref, zero_ref, w_rest_ref, w_zero_ref, out_ref):
    total = jnp.dot(w_rest_ref[...], rest_ref[...], preferred_element_type=F32)
    total += jnp.dot(w_zero_ref[...], zero_ref[:, :share], preferred_element_type=F32)
    out_ref[...] = total.astype(BF16)


def mix(rest, zero, w_rest, w_zero):
    share = rest.shape[1]
    return pl.pallas_call(
        functools.partial(mix_kernel, share),
        in_specs=[vmem()] * 4,
        out_specs=vmem(),
        out_shape=jax.ShapeDtypeStruct((w_rest.shape[0], share), BF16),
        name="mix",
    )(rest, zero, w_rest, w_zero)


def join_kernel(in0_ref, in1_ref, out_ref):
    out_ref[:, 0] = in0_ref[0]
    out_ref[:, 1] = in1_ref[0]


def join(part0, part1):
    shares, local, levels, share = part0.shape
    spec = pl.BlockSpec((1, local, levels, share), lambda q: (q, 0, 0, 0))
    return pl.pallas_call(
        join_kernel,
        grid=(shares,),
        in_specs=[spec, spec],
        out_specs=pl.BlockSpec((local, 2, levels, share), lambda q: (0, 0, 0, q)),
        out_shape=jax.ShapeDtypeStruct((local, 2, levels, shares * share), BF16),
        name="join",
    )(part0, part1)


def move_kernel(pred_ref, req_ref, w_ref, out_ref):
    sources, rows, _ = pred_ref.shape
    out_ref[...] = jnp.zeros_like(out_ref)

    def one_source(s, carry):
        amount = block_count(req_ref[s, 7:8, :])

        def one_block(b, c):
            lanes = pl.ds(pl.multiple_of(b * LANES, LANES), LANES)
            moved = jnp.dot(w_ref[...], pred_ref[s, :, lanes], precision=HIGHEST, preferred_element_type=F32)
            out_ref[s, :, lanes] = moved.astype(BF16)
            return c

        lax.fori_loop(0, amount, one_block, 0)
        return carry

    lax.fori_loop(0, sources, one_source, 0)


def move(pred, requests, w_pos):
    return pl.pallas_call(
        move_kernel,
        in_specs=[vmem()] * 3,
        out_specs=vmem(),
        out_shape=jax.ShapeDtypeStruct(pred.shape, BF16),
        name="move",
    )(pred, requests, w_pos)


def settle_kernel(back_ref, where_ref, count_ref, out_ref, acc_ref):
    tiles, rows, capacity = back_ref.shape
    drifters = where_ref.shape[1]
    acc_ref[...] = jnp.zeros_like(acc_ref)
    where_to = where_ref[...]

    def one_tile(t, carry):
        amount = block_count(count_ref[pl.ds(t, 1), :])

        def one_block(b, c):
            lanes = pl.ds(pl.multiple_of(b * LANES, LANES), LANES)
            slot = iota((LANES, drifters), 0) + (t * capacity + b * LANES)
            hit = ones_where(slot == where_to)
            acc_ref[...] += jnp.dot(back_ref[t, :, lanes], hit, preferred_element_type=F32)
            return c

        lax.fori_loop(0, amount, one_block, 0)
        return carry

    lax.fori_loop(0, tiles, one_tile, 0)
    out_ref[...] = acc_ref[...].astype(BF16)


def settle(back, where_to, count):
    _, rows, _ = back.shape
    drifters = where_to.shape[1]
    return pl.pallas_call(
        settle_kernel,
        in_specs=[vmem()] * 3,
        out_specs=vmem(),
        out_shape=jax.ShapeDtypeStruct((rows, drifters), BF16),
        scratch_shapes=[pltpu.VMEM((rows, drifters), F32)],
        name="settle",
    )(back, where_to, count)


def exchange(x, axis):
    return lax.all_to_all(x, axis, split_axis=0, concat_axis=0, tiled=True)


def shards(velocity, start_frac, observed, obs_sd, tile_of, cell_of):
    local, _, levels, cells = velocity.shape
    drifters = cell_of.shape[0]
    tiles = lax.axis_size("tile")
    shares = lax.axis_size("mem")
    members = local * shares
    share = cells // shares
    blocks = pl.cdiv(2 * drifters // tiles, LANES)

    zero, rest0, rest1 = pack(velocity, shares)
    zero = exchange(zero, "mem").reshape(2 * members, share + LANES)
    requests, where_to, count = route(
        lax.axis_index("mem"), tile_of, cell_of, start_frac, observed, obs_sd, tiles, blocks, share
    )
    requests = exchange(requests, "tile")
    rest0 = exchange(rest0, "mem").reshape(members * (levels - 1), share)
    rest1 = exchange(rest1, "mem").reshape(members * (levels - 1), share)
    pred, gram = observe(zero, requests, members, local)
    gram = all_sum(gram)
    weights = ensemble_weights(gram[:, :members], gram[:, members])
    w_rest, w_zero0, w_zero1, w_pos = spread_weights(weights, local, levels)

    mixed0 = mix(rest0, zero, w_rest, w_zero0).reshape(shares, local, levels, share)
    mixed0 = exchange(mixed0, "mem")
    moved = exchange(move(pred, requests, w_pos), "tile")
    mixed1 = mix(rest1, zero, w_rest, w_zero1).reshape(shares, local, levels, share)
    mixed1 = exchange(mixed1, "mem")
    settled = settle(moved, where_to, count).reshape(shares, 2 * local, drifters)
    settled = exchange(settled, "mem")
    new_positions = jnp.sum(settled.astype(F32), axis=0).reshape(local, 2, drifters)
    return join(mixed0, mixed1), new_positions


def solution(mesh):
    in_specs = (
        P("mem", None, None, "tile"),
        P(None, "tile"),
        P(None, "tile"),
        P("tile"),
        P("tile", None),
        P("tile"),
    )
    out_specs = (P("mem", None, None, "tile"), P("mem", None, "tile"))
    return jax.shard_map(shards, mesh=mesh, in_specs=in_specs, out_specs=out_specs, check_vma=False)
```

```python
import functools
import math

import jax
import jax.numpy as jnp
from jax import lax
from jax.experimental import pallas as pl
from jax.experimental.pallas import tpu as pltpu
from jax.sharding import PartitionSpec as P


BX = 64
LANES = 128
STEP = 0.2
BF16 = jnp.bfloat16
F32 = jnp.float32
I32 = jnp.int32
HIGHEST = lax.Precision.HIGHEST
NT = (((1,), (1,)), ((), ()))


def iota(shape, dim):
    return lax.broadcasted_iota(I32, shape, dim)


def quotient(values, divisor):
    return ((values.astype(F32) + 0.5) * (1.0 / divisor)).astype(I32)


def ones_where(mask, dtype=BF16):
    return jnp.where(mask, 1.0, 0.0).astype(dtype)


def vmem():
    return pl.BlockSpec(memory_space=pltpu.VMEM)


def smem():
    return pl.BlockSpec(memory_space=pltpu.SMEM)


def round_up(value, unit):
    return pl.cdiv(value, unit) * unit


def pack_zero_kernel(local, levels, share, z_ref, v_ref, *out_refs):
    rows, cells = v_ref.shape
    i = iota((2 * local, rows), 0)
    j = iota((2 * local, rows), 1)
    comp = (i >= local).astype(I32)
    pick = ones_where(j == ((i - comp * local) * 2 + comp) * levels)
    for r, ref in enumerate(out_refs):
        start = (z_ref[0] ^ r) * share
        after = jnp.minimum(start + share, cells - LANES)
        x = v_ref[:, pl.ds(pl.multiple_of(start, LANES), share)]
        ref[:, :share] = jnp.dot(pick, x, preferred_element_type=F32).astype(BF16)
        x = v_ref[:, pl.ds(pl.multiple_of(after, LANES), LANES)]
        ref[:, share:] = jnp.dot(pick, x, preferred_element_type=F32).astype(BF16)


def pack_rest_kernel(local, levels, share, comp, z_ref, v_ref, *out_refs):
    rows, _ = v_ref.shape
    other = levels - 1
    i = iota((other * local, rows), 0)
    j = iota((other * local, rows), 1)
    member = quotient(i, other)
    pick = ones_where(j == (member * 2 + comp) * levels + (i - member * other) + 1)
    for r, ref in enumerate(out_refs):
        start = (z_ref[0] ^ r) * share
        x = v_ref[:, pl.ds(pl.multiple_of(start, LANES), share)]
        ref[...] = jnp.dot(pick, x, preferred_element_type=F32).astype(BF16)


def pack(z, velocity, shares):
    local, _, levels, cells = velocity.shape
    share = cells // shares
    flat = velocity.reshape(local * 2 * levels, cells)
    other = (levels - 1) * local

    def call(kernel, shape):
        return pl.pallas_call(
            kernel,
            in_specs=[smem(), vmem()],
            out_specs=[vmem()] * shares,
            out_shape=[jax.ShapeDtypeStruct(shape, BF16)] * shares,
        )(z, flat)

    zero = call(functools.partial(pack_zero_kernel, local, levels, share), (2 * local, share + LANES))
    rest = [call(functools.partial(pack_rest_kernel, local, levels, share, c), (other, share)) for c in range(2)]
    return zero, rest


def route_kernel(tiles, blocks, share, q_ref, tile_ref, cell_ref, frac_ref, obs_ref, sd_ref, req_ref, where_ref, count_ref):
    drifters = cell_ref.shape[1]
    dest = tile_ref[...]
    local_cell = cell_ref[...] - q_ref[0] * share
    mine = jnp.logical_and(local_cell >= 0, local_cell < share)
    named = jnp.where(jnp.logical_and(iota((tiles, drifters), 0) == dest, mine), 1.0, 0.0)
    upper = ones_where(iota((LANES, LANES), 0) <= iota((LANES, LANES), 1))
    before = jnp.zeros((tiles, 1), F32)
    sums = []
    for start in range(0, drifters, LANES):
        part = named[:, start : start + LANES]
        sums.append(jnp.dot(part.astype(BF16), upper, preferred_element_type=F32) + before)
        before = before + jnp.sum(part, axis=1, keepdims=True)
    running = jnp.concatenate(sums, axis=1)
    slot = jnp.sum(named * (running - 1.0), axis=0, keepdims=True).astype(I32)
    total = jnp.sum(named * before, axis=0, keepdims=True)
    where_to = jnp.where(mine, dest * (blocks * LANES) + slot, -1)
    where_ref[...] = where_to
    count_ref[...] = jnp.broadcast_to(before, count_ref.shape)
    payload = jnp.concatenate(
        [local_cell.astype(F32), frac_ref[...], obs_ref[...], sd_ref[...], jnp.ones_like(total), total], axis=0
    )
    high = lax.shift_right_arithmetic(where_to, int(math.log2(LANES)))
    low = jnp.bitwise_and(where_to, LANES - 1)
    spread = jnp.concatenate([jnp.where(high == h, payload, 0.0) for h in range(tiles * blocks)], axis=0)
    place = ones_where(iota((LANES, drifters), 0) == low, F32)
    placed = lax.dot_general(spread, place, NT, precision=HIGHEST, preferred_element_type=F32)
    per = 8 * blocks
    for t in range(tiles):
        req_ref[t] = placed[t * per : (t + 1) * per]


def route(q, tile_of, cell_of, start_frac, observed, obs_sd, tiles, blocks, share):
    drifters = cell_of.shape[0]
    return pl.pallas_call(
        functools.partial(route_kernel, tiles, blocks, share),
        in_specs=[smem()] + [vmem()] * 5,
        out_specs=[vmem()] * 3,
        out_shape=[
            jax.ShapeDtypeStruct((tiles, 8 * blocks, LANES), F32),
            jax.ShapeDtypeStruct((1, drifters), I32),
            jax.ShapeDtypeStruct((tiles, LANES), F32),
        ],
        name="route",
    )(
        q,
        tile_of.reshape(1, drifters),
        cell_of.reshape(1, drifters),
        start_frac,
        observed,
        obs_sd.reshape(1, drifters),
    )


def bilinear(corner, x, y):
    return (1.0 - x) * (1.0 - y) * corner[0] + x * (1.0 - y) * corner[1] + (1.0 - x) * y * corner[2] + x * y * corner[3]


def block_count(value):
    return lax.shift_right_arithmetic(jnp.max(value).astype(I32) + (LANES - 1), int(math.log2(LANES)))


def observe_kernel(members, local, z_ref, req_ref, *refs):
    zero_refs, (pred_ref, gram_ref, table_ref, corner_ref) = refs[:-4], refs[-4:]
    sources = req_ref.shape[0]
    rows, width = 2 * members, zero_refs[0].shape[1]
    i = iota((rows, 2 * local), 0)
    j = iota((rows, 2 * local), 1)
    comp = (j >= local).astype(I32)
    target = comp * members + j - comp * local
    table = jnp.zeros((rows, width), F32)
    for r, ref in enumerate(zero_refs):
        pick = ones_where(i == target + (z_ref[0] ^ r) * local)
        table += jnp.dot(pick, ref[...], preferred_element_type=F32)
    for n, offset in enumerate((0, 1, BX, BX + 1)):
        moved = table if offset == 0 else pltpu.roll(table, width - offset, 1)
        table_ref[n * rows : (n + 1) * rows, :] = moved.astype(BF16)
    gram_ref[...] = jnp.zeros_like(gram_ref)
    spread = math.sqrt(members - 1)

    def one_block(s, b):
        r = req_ref[s, pl.ds(pl.multiple_of(b * 8, 8), 8), :]
        cell = r[0:1].astype(I32)
        hit = ones_where(iota((width, LANES), 0) == cell)
        corner_ref[...] = jnp.dot(table_ref[...], hit, preferred_element_type=F32)
        cx = [corner_ref[n * rows : n * rows + members, :] for n in range(4)]
        cy = [corner_ref[n * rows + members : (n + 1) * rows, :] for n in range(4)]
        x = jnp.broadcast_to(r[1:2], (members, LANES))
        y = jnp.broadcast_to(r[2:3], (members, LANES))
        for _ in range(2):
            mx = x + 0.5 * STEP * bilinear(cx, x, y)
            my = y + 0.5 * STEP * bilinear(cy, x, y)
            x = x + STEP * bilinear(cx, mx, my)
            y = y + STEP * bilinear(cy, mx, my)
        lanes = pl.ds(pl.multiple_of(b * LANES, LANES), LANES)
        pred_ref[s, 0:members, lanes] = x
        pred_ref[s, members:rows, lanes] = y
        valid = r[6:7] > 0.5
        deviation = jnp.where(valid, r[5:6], 1.0)
        scale = jnp.where(valid, 1.0 / (deviation * spread), 0.0)
        inverse = jnp.where(valid, 1.0 / deviation, 0.0)
        mean_x = jnp.sum(x, axis=0, keepdims=True) * (1.0 / members)
        mean_y = jnp.sum(y, axis=0, keepdims=True) * (1.0 / members)
        anomaly = jnp.concatenate([(x - mean_x) * scale, (y - mean_y) * scale], axis=1)
        innovation = jnp.concatenate([(r[3:4] - mean_x) * inverse, (r[4:5] - mean_y) * inverse], axis=1)
        first = iota((8, 2 * LANES), 0) == 0
        both = jnp.concatenate([anomaly, jnp.where(first, innovation, 0.0)], axis=0)
        gram_ref[:, 0 : members + 8] += lax.dot_general(anomaly, both, NT, precision=HIGHEST, preferred_element_type=F32)

    def one_source(s, carry):
        amount = block_count(req_ref[s, 7:8, :])
        lax.fori_loop(0, amount, lambda b, c: (one_block(s, b), c)[1], 0)
        return carry

    lax.fori_loop(0, sources, one_source, 0)


def observe(z, zero, requests, members, local):
    sources, per, _ = requests.shape
    rows, width = 2 * members, zero[0].shape[1]
    return pl.pallas_call(
        functools.partial(observe_kernel, members, local),
        in_specs=[smem()] + [vmem()] * (1 + len(zero)),
        out_specs=[vmem()] * 2,
        out_shape=[
            jax.ShapeDtypeStruct((sources, rows, per // 8 * LANES), F32),
            jax.ShapeDtypeStruct((members, LANES), F32),
        ],
        scratch_shapes=[pltpu.VMEM((4 * rows, width), BF16), pltpu.VMEM((4 * rows, LANES), F32)],
        name="observe",
    )(z, requests, *zero)


def all_sum(x):
    for axis in ("tile", "mem"):
        size = lax.axis_size(axis)
        bit = 1
        while bit < size:
            if size // bit >= 4 and not (axis == "tile" and bit == 1):
                a, b, c = [lax.ppermute(x, axis, [(n, n ^ (bit * k)) for n in range(size)]) for k in (1, 2, 3)]
                x = (x + a) + (b + c)
                bit *= 4
            else:
                x = x + lax.ppermute(x, axis, [(n, n ^ bit) for n in range(size)])
                bit *= 2
    return x


def ensemble_weights(gram_matrix, projection):
    members = gram_matrix.shape[0]
    identity = jnp.eye(members, dtype=F32)
    factor = jnp.linalg.cholesky(identity + gram_matrix)
    half_solve = lax.linalg.triangular_solve(factor, projection[:, None], left_side=True, lower=True)
    mean_weight = lax.linalg.triangular_solve(factor, half_solve, left_side=True, lower=True, transpose_a=True)
    inverse_root = lax.linalg.triangular_solve(factor, identity, left_side=True, lower=True, transpose_a=True)
    combined = mean_weight + jnp.sqrt(F32(members - 1)) * inverse_root
    return combined - jnp.mean(combined, axis=0, keepdims=True) + 1.0 / members


def spread_kernel(members, local, levels, gap, z_ref, w_ref, mix0_ref, mix1_ref, pos_ref):
    z = z_ref[0]
    other = levels - 1
    weights = w_ref[...]

    def member_of(index, each):
        r = quotient(index, local * each)
        inside = quotient(index - r * local * each, each)
        return (r ^ z) * local + inside

    rows = members * levels
    i = iota((rows, members), 0)
    repeat = ones_where(member_of(i, levels) == iota((rows, members), 1))
    tall = lax.dot_general(repeat, weights.astype(BF16), NT, preferred_element_type=F32).astype(BF16)
    shares, _, cols = mix0_ref.shape
    i = iota((rows, cols), 0)
    j = iota((rows, cols), 1)
    level = i - quotient(i, levels) * levels
    in_rest = j < other * local
    same = jnp.logical_and(in_rest, level == j - quotient(j, other) * other + 1)
    zero = jnp.logical_and(j >= gap, level == 0)
    k = iota((members, cols), 0)
    j = iota((members, cols), 1)
    for c, ref in enumerate((mix0_ref, mix1_ref)):
        offset = gap + c * local
        ours = jnp.where(j < other * local, quotient(j, other), jnp.where(j >= offset, j - offset, -members))
        ours = jnp.where(jnp.logical_and(ours >= 0, ours < local), ours, -members)
        for s in range(shares):
            widen = ones_where(k == ours + (s ^ z) * local)
            wide = jnp.dot(tall, widen, preferred_element_type=F32)
            ref[s] = jnp.where(jnp.logical_or(same, zero), wide, 0.0).astype(BF16)
    i = iota((2 * members, members), 0)
    repeat = ones_where(member_of(i, 2) == iota((2 * members, members), 1), F32)
    tall = lax.dot_general(repeat, weights, NT, precision=HIGHEST, preferred_element_type=F32)
    odd = i - 2 * quotient(i, 2) == 1
    pos_ref[:, :members] = jnp.where(odd, 0.0, tall)
    pos_ref[:, members:] = jnp.where(odd, tall, 0.0)


def mix_sizes(local, levels):
    gap = round_up(local * (levels - 1), 16)
    return gap, round_up(gap + 2 * local, 16)


def spread_weights(z, weights, local, levels):
    members = weights.shape[0]
    rows = members * levels
    gap, cols = mix_sizes(local, levels)
    return pl.pallas_call(
        functools.partial(spread_kernel, members, local, levels, gap),
        in_specs=[smem(), vmem()],
        out_specs=[vmem()] * 3,
        out_shape=[
            jax.ShapeDtypeStruct((members // local, rows, cols), BF16),
            jax.ShapeDtypeStruct((members // local, rows, cols), BF16),
            jax.ShapeDtypeStruct((2 * members, 2 * members), F32),
        ],
        name="spread",
    )(z, weights)


def mix_kernel(shares, gap, w_ref, *refs):
    rest_refs, zero_refs, out_refs, both_ref = refs[:shares], refs[shares : 2 * shares], refs[2 * shares : -1], refs[-1]
    rest_rows, share = rest_refs[0].shape
    zero_rows = zero_refs[0].shape[0]
    both_ref[...] = jnp.zeros_like(both_ref)
    for s in range(shares):
        both_ref[s, :rest_rows, :] = rest_refs[s][...]
        both_ref[s, gap : gap + zero_rows, :] = zero_refs[s][:, :share]
    rows = out_refs[0].shape[0]
    for r in range(shares):
        total = jnp.zeros((rows, share), F32)
        for s in range(shares):
            total += jnp.dot(w_ref[s, r * rows : (r + 1) * rows, :], both_ref[s], preferred_element_type=F32)
        out_refs[r][...] = total.astype(BF16)


def mix(rest, zero, weights, local, levels):
    shares, rows, cols = weights.shape
    share = rest[0].shape[1]
    gap, _ = mix_sizes(local, levels)
    return pl.pallas_call(
        functools.partial(mix_kernel, shares, gap),
        in_specs=[vmem()] * (1 + 2 * shares),
        out_specs=[vmem()] * shares,
        out_shape=[jax.ShapeDtypeStruct((rows // shares, share), BF16)] * shares,
        scratch_shapes=[pltpu.VMEM((shares, cols, share), BF16)],
        name="mix",
    )(weights, *rest, *zero)


def join_kernel(shares, z_ref, *refs):
    out_ref = refs[-1]
    share = refs[0].shape[2]
    for r in range(shares):
        start = pl.multiple_of((z_ref[0] ^ r) * share, LANES)
        out_ref[:, 0, :, pl.ds(start, share)] = refs[r][...]


def join(z, pieces, comp, levels, earlier=None):
    shares = len(pieces)
    rows, share = pieces[0].shape
    local = rows // levels
    pieces = [p.reshape(local, levels, share) for p in pieces]
    more = [] if earlier is None else [earlier]
    return pl.pallas_call(
        functools.partial(join_kernel, shares),
        grid=(1,),
        in_specs=[smem()]
        + [pl.BlockSpec((local, levels, share), lambda n: (0, 0, 0))] * shares
        + [pl.BlockSpec(memory_space=pl.ANY)] * len(more),
        out_specs=pl.BlockSpec((local, 1, levels, shares * share), lambda n: (0, comp, 0, 0)),
        out_shape=jax.ShapeDtypeStruct((local, 2, levels, shares * share), BF16),
        input_output_aliases={1 + shares: 0} if more else {},
        name="join",
    )(z, *pieces, *more)


def move_kernel(pred_ref, req_ref, w_ref, out_ref):
    sources, _, _ = pred_ref.shape
    out_ref[...] = jnp.zeros_like(out_ref)

    def one_source(s, carry):
        amount = block_count(req_ref[s, 7:8, :])

        def one_block(b, c):
            lanes = pl.ds(pl.multiple_of(b * LANES, LANES), LANES)
            moved = jnp.dot(w_ref[...], pred_ref[s, :, lanes], precision=HIGHEST, preferred_element_type=F32)
            out_ref[s, :, lanes] = moved.astype(BF16)
            return c

        lax.fori_loop(0, amount, one_block, 0)
        return carry

    lax.fori_loop(0, sources, one_source, 0)


def move(pred, requests, w_pos):
    return pl.pallas_call(
        move_kernel,
        in_specs=[vmem()] * 3,
        out_specs=vmem(),
        out_shape=jax.ShapeDtypeStruct(pred.shape, BF16),
        name="move",
    )(pred, requests, w_pos)


def settle_kernel(back_ref, where_ref, count_ref, keep_ref, send_ref, acc_ref):
    tiles, _, capacity = back_ref.shape
    drifters = where_ref.shape[1]
    acc_ref[...] = jnp.zeros_like(acc_ref)
    where_to = where_ref[...]

    def one_tile(t, carry):
        amount = block_count(count_ref[pl.ds(t, 1), :])

        def one_block(b, c):
            lanes = pl.ds(pl.multiple_of(b * LANES, LANES), LANES)
            slot = iota((LANES, drifters), 0) + (t * capacity + b * LANES)
            hit = ones_where(slot == where_to)
            acc_ref[...] += jnp.dot(back_ref[t, :, lanes], hit, preferred_element_type=F32)
            return c

        lax.fori_loop(0, amount, one_block, 0)
        return carry

    lax.fori_loop(0, tiles, one_tile, 0)
    each = keep_ref.shape[1]
    for h in range(keep_ref.shape[0]):
        keep_ref[h] = acc_ref[2 * h * each : (2 * h + 1) * each, :].astype(BF16)
        send_ref[h] = acc_ref[(2 * h + 1) * each : (2 * h + 2) * each, :].astype(BF16)


def settle(back, where_to, count, shares):
    _, rows, _ = back.shape
    drifters = where_to.shape[1]
    return pl.pallas_call(
        settle_kernel,
        in_specs=[vmem()] * 3,
        out_specs=[vmem()] * 2,
        out_shape=[jax.ShapeDtypeStruct((shares // 2, rows // shares, drifters), BF16)] * 2,
        scratch_shapes=[pltpu.VMEM((rows, drifters), F32)],
        name="settle",
    )(back, where_to, count)


def exchange(x, axis):
    return lax.all_to_all(x, axis, split_axis=0, concat_axis=0, tiled=True)


def swap(x, axis, bits):
    return lax.ppermute(x, axis, [(n, n ^ bits) for n in range(lax.axis_size(axis))])


def trade(pieces, axis):
    got = [pieces[0]]
    for r in range(1, len(pieces)):
        got.append(swap(pieces[r], axis, r))
    return got


def after(pieces, other):
    return lax.optimization_barrier((pieces, other))[0]


def assimilate(velocity, start_frac, observed, obs_sd, tile_of, cell_of):
    local, _, levels, cells = velocity.shape
    drifters = cell_of.shape[0]
    tiles = lax.axis_size("tile")
    shares = lax.axis_size("mem")
    members = local * shares
    share = cells // shares
    blocks = pl.cdiv(2 * drifters // tiles, LANES)
    z = lax.axis_index("mem").astype(I32).reshape(1)

    zero, (rest0, rest1) = pack(z, velocity, shares)
    zero = trade(zero, "mem")
    requests, where_to, count = route(z, tile_of, cell_of, start_frac, observed, obs_sd, tiles, blocks, share)
    requests = exchange(requests, "tile")
    rest0 = trade(rest0, "mem")
    pred, gram = observe(z, zero, requests, members, local)
    gram = all_sum(gram)
    rest1 = trade(after(rest1, gram), "mem")
    weights = ensemble_weights(gram[:, :members], gram[:, members])
    w_mix0, w_mix1, w_pos = spread_weights(z, weights, local, levels)

    mixed0 = trade(mix(rest0, zero, w_mix0, local, levels), "mem")
    mixed1 = trade(mix(rest1, zero, w_mix1, local, levels), "mem")
    moved = exchange(move(pred, requests, w_pos), "tile")
    keep, send = settle(moved, where_to, count, shares)
    settled = keep + swap(send, "mem", 1)
    bits = 2
    while bits < shares:
        settled = settled[0::2] + swap(settled[1::2], "mem", bits)
        bits *= 2
    new_positions = settled[0].astype(F32).reshape(local, 2, drifters)
    new_velocity = join(z, mixed0, 0, levels)
    new_velocity = join(z, mixed1, 1, levels, new_velocity)
    return new_velocity, new_positions


def solution(mesh):
    in_specs = (
        P("mem", None, None, "tile"),
        P(None, "tile"),
        P(None, "tile"),
        P("tile"),
        P("tile", None),
        P("tile"),
    )
    out_specs = (P("mem", None, None, "tile"), P("mem", None, "tile"))
    return jax.shard_map(assimilate, mesh=mesh, in_specs=in_specs, out_specs=out_specs, check_vma=False)
```

```python
import functools
import math

import jax
import jax.numpy as jnp
from jax import lax
from jax.experimental import pallas as pl
from jax.experimental.pallas import tpu as pltpu
from jax.sharding import PartitionSpec as P


BX = 64
LANES = 128
STEP = 0.2
BF16 = jnp.bfloat16
F32 = jnp.float32
I32 = jnp.int32
HIGHEST = lax.Precision.HIGHEST
NT = (((1,), (1,)), ((), ()))
TN = (((0,), (0,)), ((), ()))


def iota(shape, dim):
    return lax.broadcasted_iota(I32, shape, dim)


def quotient(values, divisor):
    return ((values.astype(F32) + 0.5) * (1.0 / divisor)).astype(I32)


def ones_where(mask, dtype=BF16):
    return jnp.where(mask, 1.0, 0.0).astype(dtype)


def vmem():
    return pl.BlockSpec(memory_space=pltpu.VMEM)


def smem():
    return pl.BlockSpec(memory_space=pltpu.SMEM)


def round_up(value, unit):
    return pl.cdiv(value, unit) * unit


def pack_zero_kernel(local, levels, share, z_ref, v_ref, *out_refs):
    rows, cells = v_ref.shape
    i = iota((2 * local, rows), 0)
    j = iota((2 * local, rows), 1)
    comp = (i >= local).astype(I32)
    pick = ones_where(j == ((i - comp * local) * 2 + comp) * levels)
    for r, ref in enumerate(out_refs):
        start = (z_ref[0] ^ r) * share
        after = jnp.minimum(start + share, cells - LANES)
        x = v_ref[:, pl.ds(pl.multiple_of(start, LANES), share)]
        ref[:, :share] = jnp.dot(pick, x, preferred_element_type=F32).astype(BF16)
        x = v_ref[:, pl.ds(pl.multiple_of(after, LANES), LANES)]
        ref[:, share:] = jnp.dot(pick, x, preferred_element_type=F32).astype(BF16)


def pack_rest_kernel(local, levels, share, comp, z_ref, v_ref, *out_refs):
    rows, _ = v_ref.shape
    other = levels - 1
    i = iota((other * local, rows), 0)
    j = iota((other * local, rows), 1)
    member = quotient(i, other)
    pick = ones_where(j == (member * 2 + comp) * levels + (i - member * other) + 1)
    for r, ref in enumerate(out_refs):
        start = (z_ref[0] ^ r) * share
        x = v_ref[:, pl.ds(pl.multiple_of(start, LANES), share)]
        ref[...] = jnp.dot(pick, x, preferred_element_type=F32).astype(BF16)


def pack(z, velocity, shares):
    local, _, levels, cells = velocity.shape
    share = cells // shares
    flat = velocity.reshape(local * 2 * levels, cells)
    other = (levels - 1) * local

    def call(kernel, shape):
        return pl.pallas_call(
            kernel,
            in_specs=[smem(), vmem()],
            out_specs=[vmem()] * shares,
            out_shape=[jax.ShapeDtypeStruct(shape, BF16)] * shares,
        )(z, flat)

    zero = call(functools.partial(pack_zero_kernel, local, levels, share), (2 * local, share + LANES))
    rest = [call(functools.partial(pack_rest_kernel, local, levels, share, c), (other, share)) for c in range(2)]
    return zero, rest


def route_kernel(tiles, blocks, share, q_ref, tile_ref, cell_ref, frac_ref, obs_ref, sd_ref, req_ref, where_ref, count_ref):
    drifters = cell_ref.shape[1]
    dest = tile_ref[...]
    local_cell = cell_ref[...] - q_ref[0] * share
    mine = jnp.logical_and(local_cell >= 0, local_cell < share)
    named = jnp.where(jnp.logical_and(iota((tiles, drifters), 0) == dest, mine), 1.0, 0.0)
    upper = ones_where(iota((LANES, LANES), 0) <= iota((LANES, LANES), 1))
    before = jnp.zeros((tiles, 1), F32)
    sums = []
    for start in range(0, drifters, LANES):
        part = named[:, start : start + LANES]
        sums.append(jnp.dot(part.astype(BF16), upper, preferred_element_type=F32) + before)
        before = before + jnp.sum(part, axis=1, keepdims=True)
    running = jnp.concatenate(sums, axis=1)
    slot = jnp.sum(named * (running - 1.0), axis=0, keepdims=True).astype(I32)
    total = jnp.sum(named * before, axis=0, keepdims=True)
    where_to = jnp.where(mine, dest * (blocks * LANES) + slot, -1)
    where_ref[...] = where_to
    count_ref[...] = jnp.broadcast_to(before, count_ref.shape)
    payload = jnp.concatenate(
        [local_cell.astype(F32), frac_ref[...], obs_ref[...], sd_ref[...], jnp.ones_like(total), total], axis=0
    )
    high = lax.shift_right_arithmetic(where_to, int(math.log2(LANES)))
    low = jnp.bitwise_and(where_to, LANES - 1)
    spread = jnp.concatenate([jnp.where(high == h, payload, 0.0) for h in range(tiles * blocks)], axis=0)
    place = ones_where(iota((LANES, drifters), 0) == low, F32)
    placed = lax.dot_general(spread, place, NT, precision=HIGHEST, preferred_element_type=F32)
    per = 8 * blocks
    for t in range(tiles):
        req_ref[t] = placed[t * per : (t + 1) * per]


def route(q, tile_of, cell_of, start_frac, observed, obs_sd, tiles, blocks, share):
    drifters = cell_of.shape[0]
    return pl.pallas_call(
        functools.partial(route_kernel, tiles, blocks, share),
        in_specs=[smem()] + [vmem()] * 5,
        out_specs=[vmem()] * 3,
        out_shape=[
            jax.ShapeDtypeStruct((tiles, 8 * blocks, LANES), F32),
            jax.ShapeDtypeStruct((1, drifters), I32),
            jax.ShapeDtypeStruct((tiles, LANES), F32),
        ],
        name="route",
    )(
        q,
        tile_of.reshape(1, drifters),
        cell_of.reshape(1, drifters),
        start_frac,
        observed,
        obs_sd.reshape(1, drifters),
    )


def bilinear(corner, x, y):
    return (1.0 - x) * (1.0 - y) * corner[0] + x * (1.0 - y) * corner[1] + (1.0 - x) * y * corner[2] + x * y * corner[3]


def block_count(value):
    return lax.shift_right_arithmetic(jnp.max(value).astype(I32) + (LANES - 1), int(math.log2(LANES)))


def observe_kernel(members, local, z_ref, req_ref, *refs):
    zero_refs, (pred_ref, gram_ref, table_ref, corner_ref) = refs[:-4], refs[-4:]
    sources = req_ref.shape[0]
    rows, width = 2 * members, zero_refs[0].shape[1]
    i = iota((rows, 2 * local), 0)
    j = iota((rows, 2 * local), 1)
    comp = (j >= local).astype(I32)
    target = comp * members + j - comp * local
    table = jnp.zeros((rows, width), F32)
    for r, ref in enumerate(zero_refs):
        pick = ones_where(i == target + (z_ref[0] ^ r) * local)
        table += jnp.dot(pick, ref[...], preferred_element_type=F32)
    for n, offset in enumerate((0, 1, BX, BX + 1)):
        moved = table if offset == 0 else pltpu.roll(table, width - offset, 1)
        table_ref[n * rows : (n + 1) * rows, :] = moved.astype(BF16)
    gram_ref[...] = jnp.zeros_like(gram_ref)
    spread = math.sqrt(members - 1)

    def one_block(s, b):
        rows_of = pl.ds(pl.multiple_of(b * 8, 8), 8)
        lanes = pl.ds(pl.multiple_of(b * LANES, LANES), LANES)
        pair = [req_ref[s, rows_of, :], req_ref[s + 1, rows_of, :]]
        cell = jnp.concatenate([r[0:1] for r in pair], axis=1).astype(I32)
        hit = ones_where(iota((width, 2 * LANES), 0) == cell)
        corner_ref[...] = jnp.dot(table_ref[...], hit, preferred_element_type=F32)
        both = []
        for h, r in enumerate(pair):
            half = slice(h * LANES, (h + 1) * LANES)
            cx = [corner_ref[n * rows : n * rows + members, half] for n in range(4)]
            cy = [corner_ref[n * rows + members : (n + 1) * rows, half] for n in range(4)]
            x = jnp.broadcast_to(r[1:2], (members, LANES))
            y = jnp.broadcast_to(r[2:3], (members, LANES))
            for _ in range(2):
                mx = x + 0.5 * STEP * bilinear(cx, x, y)
                my = y + 0.5 * STEP * bilinear(cy, x, y)
                x, y = x + STEP * bilinear(cx, mx, my), y + STEP * bilinear(cy, mx, my)
            pred_ref[s + h, 0:members, lanes] = x
            pred_ref[s + h, members:rows, lanes] = y
            valid = r[6:7] > 0.5
            deviation = jnp.where(valid, r[5:6], 1.0)
            scale = jnp.where(valid, 1.0 / (deviation * spread), 0.0)
            inverse = jnp.where(valid, 1.0 / deviation, 0.0)
            for values, seen in ((x, r[3:4]), (y, r[4:5])):
                mean = jnp.sum(values, axis=0, keepdims=True) * (1.0 / members)
                first = iota((8, LANES), 0) == 0
                last = jnp.where(first, (seen - mean) * inverse, 0.0)
                both.append(jnp.concatenate([(values - mean) * scale, last], axis=0))
        both = jnp.concatenate(both, axis=1)
        gram_ref[:, 0 : members + 8] += lax.dot_general(
            both[:members], both, NT, precision=HIGHEST, preferred_element_type=F32
        )

    def one_pair(n, carry):
        amount = jnp.maximum(block_count(req_ref[2 * n, 7:8, :]), block_count(req_ref[2 * n + 1, 7:8, :]))
        lax.fori_loop(0, amount, lambda b, c: (one_block(2 * n, b), c)[1], 0)
        return carry

    lax.fori_loop(0, sources // 2, one_pair, 0)


def observe(z, zero, requests, members, local):
    sources, per, _ = requests.shape
    rows, width = 2 * members, zero[0].shape[1]
    return pl.pallas_call(
        functools.partial(observe_kernel, members, local),
        in_specs=[smem()] + [vmem()] * (1 + len(zero)),
        out_specs=[vmem()] * 2,
        out_shape=[
            jax.ShapeDtypeStruct((sources, rows, per // 8 * LANES), F32),
            jax.ShapeDtypeStruct((members, LANES), F32),
        ],
        scratch_shapes=[pltpu.VMEM((4 * rows, width), BF16), pltpu.VMEM((4 * rows, 2 * LANES), F32)],
        name="observe",
    )(z, requests, *zero)


def all_sum_parts(x):
    parts = [x]
    for axis in ("tile", "mem"):
        size = lax.axis_size(axis)
        bit = 1
        while bit < size:
            x = parts[0] if len(parts) == 1 else add_parts(parts)
            many = 4 if size // bit >= 4 and not (axis == "tile" and bit == 1) else 2
            parts = [x] + [swap(x, axis, bit * k) for k in range(1, many)]
            bit *= many
    return parts


def add_parts(parts):
    while len(parts) > 1:
        parts = [a + b for a, b in zip(parts[0::2], parts[1::2])]
    return parts[0]


def eliminate(matrix):
    members, lanes = matrix.shape
    tiles = [matrix[n : n + 8] for n in range(0, members, 8)]
    pivots = [jnp.ones((8, lanes), F32) for _ in tiles]
    sub = iota((8, lanes), 0)
    lane = iota((8, lanes), 1)
    for j in range(members):
        at, inside = j // 8, j % 8
        source = tiles[at][inside : inside + 1]
        pivot = jnp.broadcast_to(source[:, j : j + 1], (8, lanes))
        row = jnp.where(lane == j, 1.0, jnp.broadcast_to(source, (8, lanes)))
        scaled = row * (1.0 / pivot)
        for n in range(at, len(tiles)):
            factor = jnp.broadcast_to(tiles[n][:, j : j + 1], (8, lanes))
            new = jnp.where(lane == j, 0.0, tiles[n]) - factor * scaled
            if n == at:
                new = jnp.where(sub > inside, new, jnp.where(sub == inside, row, tiles[n]))
            tiles[n] = new
        pivots[at] = jnp.where(sub == inside, pivot, pivots[at])
    return jnp.concatenate(tiles, axis=0), jnp.concatenate(pivots, axis=0)


def ensemble_weights(gram):
    members, lanes = gram.shape
    i = iota((members, lanes), 0)
    j = iota((members, lanes), 1)
    lower, pivots = eliminate(gram + jnp.where(i == j, 1.0, 0.0))
    half = lower * lax.rsqrt(pivots)
    inverse = jnp.where(j <= i, half, 0.0)[:, :members]
    mean = lax.dot_general(half, inverse, TN, precision=HIGHEST, preferred_element_type=F32)[members : members + 1]
    combined = mean + math.sqrt(members - 1) * inverse
    return combined - jnp.mean(combined, axis=1, keepdims=True) + 1.0 / members


def spread_kernel(members, local, levels, gap, z_ref, *refs):
    gram_refs, (mix0_ref, mix1_ref, pos_ref) = refs[:-3], refs[-3:]
    z = z_ref[0]
    other = levels - 1
    weights = ensemble_weights(add_parts([ref[...] for ref in gram_refs]))

    def member_of(index, each):
        r = quotient(index, local * each)
        inside = quotient(index - r * local * each, each)
        return (r ^ z) * local + inside

    rows = members * levels
    i = iota((rows, members), 0)
    repeat = ones_where(member_of(i, levels) == iota((rows, members), 1))
    tall = jnp.dot(repeat, weights.astype(BF16), preferred_element_type=F32).astype(BF16)
    shares, _, cols = mix0_ref.shape
    i = iota((rows, cols), 0)
    j = iota((rows, cols), 1)
    level = i - quotient(i, levels) * levels
    in_rest = j < other * local
    same = jnp.logical_and(in_rest, level == j - quotient(j, other) * other + 1)
    zero = jnp.logical_and(j >= gap, level == 0)
    k = iota((members, cols), 0)
    j = iota((members, cols), 1)
    for c, ref in enumerate((mix0_ref, mix1_ref)):
        offset = gap + c * local
        ours = jnp.where(j < other * local, quotient(j, other), jnp.where(j >= offset, j - offset, -members))
        ours = jnp.where(jnp.logical_and(ours >= 0, ours < local), ours, -members)
        for s in range(shares):
            widen = ones_where(k == ours + (s ^ z) * local)
            wide = jnp.dot(tall, widen, preferred_element_type=F32)
            ref[s] = jnp.where(jnp.logical_or(same, zero), wide, 0.0).astype(BF16)
    i = iota((2 * members, members), 0)
    repeat = ones_where(member_of(i, 2) == iota((2 * members, members), 1), F32)
    tall = jnp.dot(repeat, weights, precision=HIGHEST, preferred_element_type=F32)
    odd = i - 2 * quotient(i, 2) == 1
    pos_ref[:, :members] = jnp.where(odd, 0.0, tall)
    pos_ref[:, members:] = jnp.where(odd, tall, 0.0)


def mix_sizes(local, levels):
    gap = round_up(local * (levels - 1), 16)
    return gap, round_up(gap + 2 * local, 16)


def spread_weights(z, gram_parts, local, levels):
    members = gram_parts[0].shape[0]
    rows = members * levels
    gap, cols = mix_sizes(local, levels)
    return pl.pallas_call(
        functools.partial(spread_kernel, members, local, levels, gap),
        in_specs=[smem()] + [vmem()] * len(gram_parts),
        out_specs=[vmem()] * 3,
        out_shape=[
            jax.ShapeDtypeStruct((members // local, rows, cols), BF16),
            jax.ShapeDtypeStruct((members // local, rows, cols), BF16),
            jax.ShapeDtypeStruct((2 * members, 2 * members), F32),
        ],
        name="spread",
    )(z, *gram_parts)


def mix_kernel(shares, gap, w_ref, *refs):
    rest_refs, zero_refs, out_refs, both_ref = refs[:shares], refs[shares : 2 * shares], refs[2 * shares : -1], refs[-1]
    rest_rows, share = rest_refs[0].shape
    zero_rows = zero_refs[0].shape[0]
    both_ref[...] = jnp.zeros_like(both_ref)
    for s in range(shares):
        both_ref[s, :rest_rows, :] = rest_refs[s][...]
        both_ref[s, gap : gap + zero_rows, :] = zero_refs[s][:, :share]
    rows = out_refs[0].shape[0]
    for r in range(shares):
        total = jnp.zeros((rows, share), F32)
        for s in range(shares):
            total += jnp.dot(w_ref[s, r * rows : (r + 1) * rows, :], both_ref[s], preferred_element_type=F32)
        out_refs[r][...] = total.astype(BF16)


def mix(rest, zero, weights, local, levels):
    shares, rows, cols = weights.shape
    share = rest[0].shape[1]
    gap, _ = mix_sizes(local, levels)
    return pl.pallas_call(
        functools.partial(mix_kernel, shares, gap),
        in_specs=[vmem()] * (1 + 2 * shares),
        out_specs=[vmem()] * shares,
        out_shape=[jax.ShapeDtypeStruct((rows // shares, share), BF16)] * shares,
        scratch_shapes=[pltpu.VMEM((shares, cols, share), BF16)],
        name="mix",
    )(weights, *rest, *zero)


def join_kernel(shares, z_ref, *refs):
    out_ref = refs[-1]
    share = refs[0].shape[2]
    for r in range(shares):
        start = pl.multiple_of((z_ref[0] ^ r) * share, LANES)
        out_ref[:, 0, :, pl.ds(start, share)] = refs[r][...]


def join(z, pieces, comp, levels, earlier=None):
    shares = len(pieces)
    rows, share = pieces[0].shape
    local = rows // levels
    pieces = [p.reshape(local, levels, share) for p in pieces]
    more = [] if earlier is None else [earlier]
    return pl.pallas_call(
        functools.partial(join_kernel, shares),
        grid=(1,),
        in_specs=[smem()]
        + [pl.BlockSpec((local, levels, share), lambda n: (0, 0, 0))] * shares
        + [pl.BlockSpec(memory_space=pl.ANY)] * len(more),
        out_specs=pl.BlockSpec((local, 1, levels, shares * share), lambda n: (0, comp, 0, 0)),
        out_shape=jax.ShapeDtypeStruct((local, 2, levels, shares * share), BF16),
        input_output_aliases={1 + shares: 0} if more else {},
        name="join",
    )(z, *pieces, *more)


def move_kernel(pred_ref, req_ref, w_ref, out_ref):
    sources, _, _ = pred_ref.shape
    out_ref[...] = jnp.zeros_like(out_ref)

    def one_pair(n, carry):
        s = 2 * n
        amount = jnp.maximum(block_count(req_ref[s, 7:8, :]), block_count(req_ref[s + 1, 7:8, :]))

        def one_block(b, c):
            lanes = pl.ds(pl.multiple_of(b * LANES, LANES), LANES)
            both = jnp.concatenate([pred_ref[s, :, lanes], pred_ref[s + 1, :, lanes]], axis=1)
            moved = jnp.dot(w_ref[...], both, precision=HIGHEST, preferred_element_type=F32).astype(BF16)
            out_ref[s, :, lanes] = moved[:, :LANES]
            out_ref[s + 1, :, lanes] = moved[:, LANES:]
            return c

        lax.fori_loop(0, amount, one_block, 0)
        return carry

    lax.fori_loop(0, sources // 2, one_pair, 0)


def move(pred, requests, w_pos):
    return pl.pallas_call(
        move_kernel,
        in_specs=[vmem()] * 3,
        out_specs=vmem(),
        out_shape=jax.ShapeDtypeStruct(pred.shape, BF16),
        name="move",
    )(pred, requests, w_pos)


def settle_kernel(back_ref, where_ref, count_ref, keep_ref, send_ref, acc_ref):
    tiles, _, capacity = back_ref.shape
    drifters = where_ref.shape[1]
    acc_ref[...] = jnp.zeros_like(acc_ref)
    where_to = where_ref[...]

    def one_tile(t, carry):
        amount = block_count(count_ref[pl.ds(t, 1), :])

        def one_block(b, c):
            lanes = pl.ds(pl.multiple_of(b * LANES, LANES), LANES)
            slot = iota((LANES, drifters), 0) + (t * capacity + b * LANES)
            hit = ones_where(slot == where_to)
            acc_ref[...] += jnp.dot(back_ref[t, :, lanes], hit, preferred_element_type=F32)
            return c

        lax.fori_loop(0, amount, one_block, 0)
        return carry

    lax.fori_loop(0, tiles, one_tile, 0)
    each = keep_ref.shape[1]
    for h in range(keep_ref.shape[0]):
        keep_ref[h] = acc_ref[2 * h * each : (2 * h + 1) * each, :].astype(BF16)
        send_ref[h] = acc_ref[(2 * h + 1) * each : (2 * h + 2) * each, :].astype(BF16)


def settle(back, where_to, count, shares):
    _, rows, _ = back.shape
    drifters = where_to.shape[1]
    return pl.pallas_call(
        settle_kernel,
        in_specs=[vmem()] * 3,
        out_specs=[vmem()] * 2,
        out_shape=[jax.ShapeDtypeStruct((shares // 2, rows // shares, drifters), BF16)] * 2,
        scratch_shapes=[pltpu.VMEM((rows, drifters), F32)],
        name="settle",
    )(back, where_to, count)


def exchange(x, axis):
    return lax.all_to_all(x, axis, split_axis=0, concat_axis=0, tiled=True)


def swap(x, axis, bits):
    return lax.ppermute(x, axis, [(n, n ^ bits) for n in range(lax.axis_size(axis))])


def trade(pieces, axis):
    got = [pieces[0]]
    for r in range(1, len(pieces)):
        got.append(swap(pieces[r], axis, r))
    return got


def assimilate(velocity, start_frac, observed, obs_sd, tile_of, cell_of):
    local, _, levels, cells = velocity.shape
    drifters = cell_of.shape[0]
    tiles = lax.axis_size("tile")
    shares = lax.axis_size("mem")
    members = local * shares
    share = cells // shares
    blocks = pl.cdiv(2 * drifters // tiles, LANES)
    z = lax.axis_index("mem").astype(I32).reshape(1)

    zero, (rest0, rest1) = pack(z, velocity, shares)
    zero = trade(zero, "mem")
    requests, where_to, count = route(z, tile_of, cell_of, start_frac, observed, obs_sd, tiles, blocks, share)
    requests = exchange(requests, "tile")
    rest0 = trade(rest0, "mem")
    pred, gram = observe(z, zero, requests, members, local)
    rest1 = trade(rest1, "mem")
    w_mix0, w_mix1, w_pos = spread_weights(z, all_sum_parts(gram), local, levels)

    mixed0 = trade(mix(rest0, zero, w_mix0, local, levels), "mem")
    mixed1 = trade(mix(rest1, zero, w_mix1, local, levels), "mem")
    moved = exchange(move(pred, requests, w_pos), "tile")
    keep, send = settle(moved, where_to, count, shares)
    settled = keep + swap(send, "mem", 1)
    bits = 2
    while bits < shares:
        settled = settled[0::2] + swap(settled[1::2], "mem", bits)
        bits *= 2
    new_positions = settled[0].astype(F32).reshape(local, 2, drifters)
    new_velocity = join(z, mixed0, 0, levels)
    new_velocity = join(z, mixed1, 1, levels, new_velocity)
    return new_velocity, new_positions


def solution(mesh):
    in_specs = (
        P("mem", None, None, "tile"),
        P(None, "tile"),
        P(None, "tile"),
        P("tile"),
        P("tile", None),
        P("tile"),
    )
    out_specs = (P("mem", None, None, "tile"), P("mem", None, "tile"))
    return jax.shard_map(assimilate, mesh=mesh, in_specs=in_specs, out_specs=out_specs, check_vma=False)
```
